1024 devices in a mesh: expert: 32 (over z_lo, x), seq: 32 (over z_hi, y, core).
Axes of the slice: x: 4, y: 8, z: 16 (z_hi: 2, z_lo: 8; z = z_hi * 8 + z_lo), core: 2. Of those that a mesh axis runs over, the one named last changes fastest.
Arguments:
- tokens: bfloat16 [131072, 2048], P(('expert', 'seq')), may hold values from -24 to 24
- out_grad: bfloat16 [131072, 2048], P(('expert', 'seq')), may hold values from -6 to 6
- expert_ids: int32 [131072, 8], P(('expert', 'seq')), may hold values from 0 to 127, all different within a row; in each aligned block of 128 rows (0 to 127, 128 to 255, ...) at most 12 rows name the same one
- combine: float32 [131072, 8], P(('expert', 'seq')), may hold values from 0.05 to 1
- w_gate: bfloat16 [32, 2048, 192], P('expert'), may hold values from -0.125 to 0.125
- w_up: bfloat16 [32, 2048, 192], P('expert'), may hold values from -0.125 to 0.125
- w_down: bfloat16 [32, 192, 2048], P('expert'), may hold values from -0.21875 to 0.21875
Outputs:
- grad_tokens: bfloat16 [131072, 2048], P(('expert', 'seq'))
- grad_combine: float32 [131072, 8], P(('expert', 'seq'))
- weight_grads: bfloat16 [32, 2048, 3, 192], P('expert', 'seq')
The draws below stay inside these ranges and needn't reach their ends.
Inputs may be any that keep to these rules, and one draw needn't show every extreme that they name: `expert_ids`: each token names 8 different experts. Among the tokens of one device no expert is named by more than 12. Slice j of the weights belongs to index j of the expert axis; only experts below 8 are held.
All inputs are finite; a program needn't handle non-finite values.
Results may differ from the reference program's by a relative error of at most 0.025.
Values may be sent and summed in bfloat16 or wider, within the bound.
No kernel may reach another device: no remote copies, remote signals or barrier semaphores. Data moves between devices by JAX's collectives and lax.ppermute only.
A program may use at most 64 MiB of HBM per device.

```python
import math
import jax
import jax.numpy as jnp
import numpy as np
from jax import lax

D = 2048
HID = 768
E_ALL = 128
TOP = 8
HSPLIT = 4
TOK_DEV = 128
CAP = 12
HPART = 192
TOKENS = 131072
N_EXPERT = 32
N_SEQ = 32


def raised(drawn, own_key, source, target, parts, factor):
    owner, partner = [(jnp.arange(drawn.shape[dim]) // (drawn.shape[dim] // parts)).reshape([-1 if axis == dim else 1 for axis in range(drawn.ndim)]) for dim in (source, target)]
    chosen = jax.random.permutation(own_key, parts)[partner]
    strong = (owner == chosen) | (owner == (partner + parts // 2) % parts)
    return jnp.where(strong, factor * drawn, drawn)


def block_scale(stream_key, dims, cuts, low, largest):
    def one(dim, blocks):
        heights = jax.random.uniform(jax.random.fold_in(jax.random.fold_in(stream_key, 6), dim), (blocks,), jnp.float32, low / len(cuts), largest / len(cuts))
        return jnp.repeat(jnp.exp(heights), dims[dim] // blocks).reshape((-1,) + (1,) * (len(dims) - dim - 1))

    loudness = one(*cuts[0])
    for cut in cuts[1:]:
        loudness = loudness * one(*cut)
    return loudness


def deal_out(stream_key, own, number, rows, number_of, top, limit, skew):
    order = jax.random.permutation(stream_key, number_of)
    crowded, ordinary = shares(number_of, rows * top, limit, skew, True), shares(number_of, rows * top, limit, skew, False)
    places = jnp.arange(number_of)

    def named(lengths, rotation):
        used = int((lengths > 0).sum())
        fixed = max(1, used // 4)
        shifted = fixed + (places - fixed + rotation * (used - fixed)) % max(1, number_of - fixed)
        return jnp.zeros((number_of,), jnp.int32).at[order[jnp.where(places < fixed, places, shifted)]].set(jnp.asarray(lengths, jnp.int32))

    lengths = jnp.where(number % 4 == 0, named(crowded, number // 4), named(ordinary, number - number // 4 - 1))
    mixed = jax.random.permutation(jax.random.fold_in(own, 3), number_of)
    donor, sink = mixed[0:number_of // 2 * 2:2], mixed[1:number_of // 2 * 2:2]
    margin = jnp.minimum(lengths[donor] - 1, limit - lengths[sink]) // 2
    margin = jnp.where((donor == order[0]) | (sink == order[0]) | (lengths[sink] == 0), 0, jnp.maximum(margin, 0))
    shifted = jax.random.randint(jax.random.fold_in(own, 4), (number_of // 2,), 0, 1 << 20) % (margin + 1)
    lengths = lengths.at[donor].add(-shifted).at[sink].add(shifted)
    items = jnp.searchsorted(jnp.cumsum(lengths), jnp.arange(rows * top), side="right").astype(jnp.int32)
    grid = items.reshape(top, rows).T
    grid = grid[jax.random.permutation(jax.random.fold_in(own, 1), rows)]
    rotation = jax.random.randint(jax.random.fold_in(own, 2), (rows, 1), 0, top)
    return jnp.take_along_axis(grid, (jnp.arange(top)[None, :] + rotation) % top, axis=1)


def shares(number_of, total, most, slope, full):
    weights = [(1 << 20) // math.isqrt(standing ** slope) + 1 for standing in range(1, number_of + 1)]
    largest = most if full else min(most, max(-(-total // number_of), total * weights[0] // sum(weights)))
    least = 1 if total - largest >= number_of - 1 else 0
    holding, spare = [largest] + [least] * (number_of - 1), total - largest - least * (number_of - 1)
    while spare > 0:
        movable = [i for i in range(1, number_of) if holding[i] < largest] or [i for i in range(1, number_of) if holding[i] < most]
        pool, budget = sum([weights[i] for i in movable]), spare
        for i in movable:
            addition = min(most - holding[i], max(1, budget * weights[i] // pool), spare)
            holding[i] = holding[i] + addition
            spare = spare - addition
    return np.array(holding)


def centred(key, shape, scale, limit, cuts=(), kind=jnp.bfloat16):
    result = jax.random.normal(key, shape, jnp.float32) * scale
    if len(cuts) > 0:
        result = block_scale(key, shape, cuts, -0.22, 0.18) * result
    return jnp.clip(result, min=-limit, max=limit).astype(kind)


def heavy_noise(stream_key, dims, scale, bound, shards, heavy, kind=jnp.bfloat16):
    entries = scale * jax.random.normal(stream_key, dims, jnp.float32)
    if shards:
        entries = entries * block_scale(stream_key, dims, shards, -0.22, 0.18)
    return jnp.clip(raised(entries, jax.random.fold_in(stream_key, 3), *heavy), -bound, bound).astype(kind)


def setup_inputs(seed: int = 0) -> dict:
    splits = jax.random.split(jax.random.key(seed), 8)
    tokens = heavy_noise(splits[0], (TOKENS, D), 1.0, 24.0, ((0, 1024),), (0, 1, 1024, 6.0))
    out_grad = centred(splits[1], (TOKENS, D), 1.0, 6.0, ((0, 1024),))
    expert_ids_keys = jax.random.split(jax.random.fold_in(splits[2], 1), TOKENS // TOK_DEV)
    expert_ids_turns = jax.random.permutation(jax.random.fold_in(splits[2], 3), TOKENS // TOK_DEV)
    expert_ids = jax.vmap(lambda own, number: deal_out(jax.random.fold_in(splits[2], 2), own, number, TOK_DEV, E_ALL, TOP, CAP, 1))(expert_ids_keys, expert_ids_turns).reshape((TOKENS, TOP))
    combine = jnp.clip(jnp.exp(math.log(1.0) - 2.9957323 * jax.random.uniform(splits[3], (TOKENS, TOP), jnp.float32) ** block_scale(splits[3], (TOKENS, TOP), ((0, 1024),), -0.2, 0.2)), 0.05, 1.0)
    w_gate = centred(splits[4], (N_EXPERT, D, HPART), D ** -0.5, 0.125, ((0, 32),))
    w_up = centred(splits[5], (N_EXPERT, D, HPART), D ** -0.5, 0.125, ((0, 32),))
    w_down = centred(splits[6], (N_EXPERT, HPART, D), HID ** -0.5, 0.21875, ((0, 32),))
    return dict(tokens=tokens, out_grad=out_grad, expert_ids=expert_ids, combine=combine, w_gate=w_gate, w_up=w_up, w_down=w_down)


def reference(tokens, out_grad, expert_ids, combine, w_gate, w_up, w_down):
    blocks = N_EXPERT * N_SEQ
    experts = N_EXPERT // HSPLIT
    slice_width = HID // HSPLIT
    tok_x = tokens.reshape(blocks, TOK_DEV, D)
    tok_g = out_grad.reshape(blocks, TOK_DEV, D)
    chosen_ids = expert_ids.reshape(blocks, TOK_DEV, TOP)
    weights = combine.reshape(blocks, TOK_DEV, TOP)
    slot_ids = jnp.arange(CAP, dtype=jnp.int32)
    places = jnp.arange(TOK_DEV, dtype=jnp.int32)
    block_ids = jnp.arange(blocks, dtype=jnp.int32)
    gate_all = w_gate.reshape(experts, HSPLIT, D, slice_width)
    up_all = w_up.reshape(experts, HSPLIT, D, slice_width)
    down_all = w_down.reshape(experts, HID, D)

    def by_seq(values):
        width = values.shape[-1]
        shaped = values.reshape(N_EXPERT, N_SEQ, CAP, width)
        return jnp.transpose(shaped, (1, 0, 2, 3)).reshape(N_SEQ, N_EXPERT * CAP, width)

    def expert_pass(state_now, expert):
        grad_tok, grad_comb = state_now
        chosen = chosen_ids == expert
        routed = jnp.any(chosen, axis=2).astype(jnp.int32)
        earlier = jnp.cumsum(routed, axis=1, dtype=jnp.int32) - routed
        picker = (earlier[:, None, :] == slot_ids[None, :, None]) & (routed[:, None, :] == 1)
        filled = jnp.any(picker, axis=2)
        where_tok = jnp.sum(jnp.where(picker, places[None, None, :], 0), axis=2).astype(jnp.int32)
        weight_te = jnp.sum(jnp.where(chosen, weights, 0.0), axis=2)
        rows_w = jnp.sum(jnp.where(picker, weight_te[:, None, :], 0.0), axis=2)
        gather_x = jnp.take_along_axis(tok_x, where_tok[:, :, None], axis=1)
        gather_g = jnp.take_along_axis(tok_g, where_tok[:, :, None], axis=1)
        rows_x = jnp.where(filled[:, :, None], gather_x, jnp.zeros_like(gather_x)).astype(jnp.bfloat16)
        rows_g = jnp.where(filled[:, :, None], gather_g, jnp.zeros_like(gather_g)).astype(jnp.bfloat16)
        gate_cols = jnp.transpose(gate_all[expert], (1, 0, 2)).reshape(D, HID)
        up_cols = jnp.transpose(up_all[expert], (1, 0, 2)).reshape(D, HID)
        down_rows = down_all[expert]
        flat_x = rows_x.reshape(-1, D)
        flat_g = rows_g.reshape(-1, D)
        flat_w = rows_w.reshape(-1)
        gate_pre = jnp.dot(flat_x, gate_cols, preferred_element_type=jnp.float32)
        up_pre = jnp.dot(flat_x, up_cols, preferred_element_type=jnp.float32)
        sig_gate = jax.nn.sigmoid(gate_pre)
        act_gate = gate_pre * sig_gate
        hidden = (act_gate * up_pre).astype(jnp.bfloat16)
        expert_out = jnp.dot(hidden, down_rows, preferred_element_type=jnp.float32)
        comb_rows = jnp.sum(flat_g.astype(jnp.float32) * expert_out, axis=1)
        scaled = (flat_w[:, None] * flat_g.astype(jnp.float32)).astype(jnp.bfloat16)
        hidden_grad = jnp.dot(scaled, down_rows.T, preferred_element_type=jnp.float32)
        grad_gate = (hidden_grad * up_pre * sig_gate * (1.0 + gate_pre * (1.0 - sig_gate))).astype(jnp.bfloat16)
        grad_up = (hidden_grad * act_gate).astype(jnp.bfloat16)
        contrib = jnp.zeros((flat_x.shape[0], D), jnp.float32)
        for slice_no in range(HSPLIT):
            lo_col = slice_no * slice_width
            hi_col = lo_col + slice_width
            piece = jnp.dot(grad_gate[:, lo_col:hi_col], gate_cols[:, lo_col:hi_col].T, preferred_element_type=jnp.float32)
            piece = piece + jnp.dot(grad_up[:, lo_col:hi_col], up_cols[:, lo_col:hi_col].T, preferred_element_type=jnp.float32)
            rounded = lax.optimization_barrier(piece.astype(jnp.bfloat16))
            contrib = contrib + rounded.astype(jnp.float32)
        contrib = contrib.reshape(blocks, CAP, D)
        contrib = jnp.where(filled[:, :, None], contrib, 0.0)
        grad_tok = grad_tok.at[block_ids[:, None], where_tok].add(contrib)
        comb_te = jnp.sum(jnp.where(picker, comb_rows.reshape(blocks, CAP)[:, :, None], 0.0), axis=1)
        grad_comb = grad_comb + jnp.where(chosen, comb_te[:, :, None], 0.0)

        def per_seq(running, pieces):
            piece_x, piece_gate, piece_up, piece_scaled, piece_hidden = pieces
            term_gate = jnp.dot(piece_x.T, piece_gate, preferred_element_type=jnp.float32)
            term_up = jnp.dot(piece_x.T, piece_up, preferred_element_type=jnp.float32)
            term_down = jnp.dot(piece_scaled.T, piece_hidden, preferred_element_type=jnp.float32)
            term_all = lax.optimization_barrier(jnp.stack([term_gate, term_up, term_down]).astype(jnp.bfloat16))
            return running + term_all.astype(jnp.float32), None

        summed, _ = lax.scan(per_seq, jnp.zeros((3, D, HID), jnp.float32),
                             (by_seq(flat_x), by_seq(grad_gate), by_seq(grad_up), by_seq(scaled), by_seq(hidden)))
        grads = summed.astype(jnp.bfloat16).reshape(3, D, HSPLIT, slice_width)
        grads = jnp.transpose(grads, (2, 1, 0, 3))
        return (grad_tok, grad_comb), grads

    start = (jnp.zeros((blocks, TOK_DEV, D), jnp.float32), jnp.zeros((blocks, TOK_DEV, TOP), jnp.float32))
    (grad_tok, grad_comb), grads = lax.scan(expert_pass, start, jnp.arange(experts, dtype=jnp.int32))
    grad_tokens = grad_tok.reshape(blocks * TOK_DEV, D).astype(jnp.bfloat16)
    grad_combine = grad_comb.reshape(blocks * TOK_DEV, TOP)
    weight_grads = grads.reshape(N_EXPERT, D, 3, slice_width)
    return (grad_tokens, grad_combine, weight_grads)
```

```python
import jax
import jax.numpy as jnp
from jax import lax
from jax.sharding import Mesh
from jax.sharding import PartitionSpec as P

D = 2048
HALF = 1024
HSPLIT = 4
CAP = 12
BF = jnp.bfloat16
F32 = jnp.float32


def dot(left, right, dims):
    return lax.dot_general(left, right, ((dims[:1], dims[1:]), ((), ())), preferred_element_type=F32)


def flip(values, axis, mask):
    size = lax.axis_size(axis)
    return lax.ppermute(values, axis, [(i, i ^ mask) for i in range(size)])


def shift(values, axis, step):
    size = lax.axis_size(axis)
    return lax.ppermute(values, axis, [(i, (i + step) % size) for i in range(size)])


def exchange(values, axis):
    return lax.all_to_all(values, axis, split_axis=0, concat_axis=0, tiled=True)


def pick(blocks, index):
    return lax.dynamic_index_in_dim(blocks, index, 0, keepdims=False)


def ring_sum(blocks):
    n = lax.axis_size("y")
    me = lax.axis_index("y")

    def mine(step):
        return pick(blocks, lax.rem(me + step + n, n)).astype(F32)

    up = down = None
    far = n // 2
    for hop in range(far, 0, -1):
        part = mine(hop) if up is None else mine(hop) + up.astype(F32)
        up = shift(part.astype(BF), "y", 1)
        if hop < far:
            part = mine(-hop) if down is None else mine(-hop) + down.astype(F32)
            down = shift(part.astype(BF), "y", -1)
    total = mine(0) + up.astype(F32)
    return total if down is None else total + down.astype(F32)


def local(tokens, out_grad, expert_ids, combine, w_gate, w_up, w_down):
    n_z = lax.axis_size("zl")
    tok_dev = tokens.shape[0]
    width = w_gate.shape[2]
    wanted = lax.broadcasted_iota(jnp.int32, (1, 1, n_z), 2)
    chosen = expert_ids[:, :, None] == wanted
    routed = jnp.any(chosen, axis=1).astype(jnp.int32)
    earlier = jnp.cumsum(routed, axis=0, dtype=jnp.int32) - routed
    slot_ids = lax.broadcasted_iota(jnp.int32, (1, CAP, 1), 1)
    picker = (earlier.T[:, None, :] == slot_ids) & (routed.T[:, None, :] == 1)
    weight_te = jnp.sum(jnp.where(chosen, combine[:, :, None], 0.0), axis=1)
    slot_w = jnp.sum(jnp.where(picker, weight_te.T[:, None, :], 0.0), axis=2)
    picker_bf = picker.astype(BF)
    blank = jnp.zeros_like(picker_bf)
    pick_x = jnp.concatenate([picker_bf, blank], axis=1).reshape(-1, tok_dev)
    pick_g = jnp.concatenate([blank, picker_bf], axis=1).reshape(-1, tok_dev)
    scale = jnp.concatenate([jnp.ones_like(slot_w), slot_w], axis=1).reshape(-1, 1)
    rows = dot(pick_x, tokens, (1, 0)) + dot(pick_g, out_grad, (1, 0))
    out_rows = (rows * scale).astype(BF).reshape(n_z, 2 * CAP, D)

    own = exchange(out_rows, "zl")
    near1 = flip(own, "x", 1)
    near3 = flip(own, "x", 3)
    half = n_z // 2
    far_a = flip(near1[:half], "x", 3)
    far_b = flip(near3[half:], "x", 1)
    flat = jnp.concatenate([own, near1, far_a, far_b, near3], axis=0).reshape(-1, D)

    cols = jnp.concatenate([w_gate[0], w_up[0], w_down[0].T], axis=1)
    pre = dot(flat, cols, (1, 0)).reshape(-1, 2 * CAP, 3 * width)
    gate_pre = pre[:, :CAP, :width]
    up_pre = pre[:, :CAP, width : 2 * width]
    hidden_grad = pre[:, CAP:, 2 * width :]
    sig_gate = jax.nn.sigmoid(gate_pre)
    act_gate = gate_pre * sig_gate
    hidden = (act_gate * up_pre).astype(BF)
    grad_gate = (hidden_grad * up_pre * sig_gate * (1.0 + gate_pre * (1.0 - sig_gate))).astype(BF)
    grad_up = (hidden_grad * act_gate).astype(BF)
    comb = jnp.sum(hidden.astype(F32) * hidden_grad, axis=2, keepdims=True)
    both = jnp.concatenate([grad_gate, grad_up], axis=2)
    right = jnp.concatenate(
        [
            jnp.pad(both, ((0, 0), (0, 0), (0, width))),
            jnp.pad(hidden, ((0, 0), (0, 0), (2 * width, 0))),
        ],
        axis=1,
    ).reshape(-1, 3 * width)
    terms = dot(flat, right, (0, 0)).astype(BF)

    n_y = lax.axis_size("y")
    n_c = lax.axis_size("c")
    n_h = lax.axis_size("zh")
    core = lax.axis_index("c")
    high = lax.axis_index("zh")
    share = D // (n_h * n_y * n_c)
    parts = terms.reshape(n_h, n_y, n_c, share, 3 * width).transpose(2, 1, 0, 3, 4)
    theirs = flip(pick(parts, 1 - core), "c", 1)
    pair = (pick(parts, core).astype(F32) + theirs.astype(F32)).astype(BF)
    line = ring_sum(pair).astype(BF)
    across = flip(pick(line, 1 - high), "zh", 1)
    summed = pick(line, high).astype(F32) + across.astype(F32)
    weight_grads = summed.astype(BF).reshape(1, share, 3, width)

    me = lax.axis_index("x")
    order = lax.bitwise_xor(jnp.arange(HSPLIT, dtype=jnp.int32), me)
    grads = both.reshape(HSPLIT, n_z * CAP, 2 * width)
    grads = jnp.stack([pick(grads, order[i]) for i in range(HSPLIT)])
    comb4 = comb.reshape(HSPLIT, n_z * CAP, 1)
    comb4 = jnp.stack([pick(comb4, order[i]) for i in range(HSPLIT)])
    back = dot(grads.reshape(-1, 2 * width), cols[:, : 2 * width], (1, 1)).astype(BF)
    back = back.reshape(HSPLIT, n_z * CAP, D)
    back = jnp.concatenate([back, jnp.pad(comb4.astype(BF), ((0, 0), (0, 0), (0, 127)))], axis=2)
    back = exchange(back, "x")
    total = jnp.sum(back.astype(F32), axis=0).astype(BF).reshape(n_z, CAP, D + 128)
    head, tail = total[:, :8], total[:, 8:]
    low = jnp.concatenate([tail[:, :, :HALF], tail[:, :, HALF:D]], axis=1)
    comb_low = jnp.pad(tail[:, :, D:], ((0, 0), (0, 4), (0, 0)))
    side = jnp.concatenate([head[:, :, D : D + 1], comb_low[:, :, :1]], axis=2)
    side = jnp.pad(side, ((0, 0), (0, 0), (0, 126)))
    packed = jnp.concatenate([head[:, :, :D], low, side], axis=2)
    ret = exchange(packed, "zl")

    first = picker_bf[:, :8].reshape(n_z * 8, tok_dev)
    last = picker_bf[:, 8:]
    none = jnp.zeros_like(last)
    last_lo = jnp.concatenate([last, none], axis=1).reshape(n_z * 8, tok_dev)
    last_hi = jnp.concatenate([none, last], axis=1).reshape(n_z * 8, tok_dev)
    flat_ret = ret.reshape(n_z * 8, -1)
    tail_ret = flat_ret[:, D : D + HALF]
    main = dot(first, flat_ret[:, :D], (0, 0))
    rest = jnp.concatenate([dot(last_lo, tail_ret, (0, 0)), dot(last_hi, tail_ret, (0, 0))], axis=1)
    grad_tokens = (main + rest).astype(BF)
    comb_slots = jnp.concatenate(
        [ret[:, :, D + HALF], ret[:, :4, D + HALF + 1]], axis=1
    ).astype(F32)
    comb_te = jnp.sum(jnp.where(picker, comb_slots[:, :, None], 0.0), axis=1)
    raw = jnp.sum(jnp.where(chosen, comb_te.T[:, None, :], 0.0), axis=2)
    here = jnp.any(chosen, axis=2)
    grad_combine = jnp.where(here, raw / jnp.where(here, combine, 1.0), 0.0)
    return (grad_tokens, grad_combine, weight_grads)


def solution(mesh):
    n_expert, n_seq = mesh.devices.shape
    grid = Mesh(
        mesh.devices.reshape(n_expert // HSPLIT, HSPLIT, 2, n_seq // 4, 2),
        ("zl", "x", "zh", "y", "c"),
    )
    expert, seq = ("zl", "x"), ("zh", "y", "c")
    tok = P(expert + seq, None)
    wgt = P(expert, None, None)
    return jax.shard_map(
        local,
        mesh=grid,
        in_specs=(tok, tok, tok, tok, wgt, wgt, wgt),
        out_specs=(tok, tok, P(expert, seq, None, None)),
        check_vma=False,
    )
```

```python
import functools

import jax
import jax.numpy as jnp
from jax import lax
from jax.experimental import pallas as pl
from jax.experimental.pallas import tpu as pltpu
from jax.sharding import Mesh
from jax.sharding import PartitionSpec as P

D = 2048
HALF = 1024
HSPLIT = 4
CAP = 12
BF = jnp.bfloat16
F32 = jnp.float32


def dot(left, right, dims):
    return lax.dot_general(left, right, ((dims[:1], dims[1:]), ((), ())), preferred_element_type=F32)


def flip(values, axis, mask):
    size = lax.axis_size(axis)
    return lax.ppermute(values, axis, [(i, i ^ mask) for i in range(size)])


def exchange(values, axis):
    return lax.all_to_all(values, axis, split_axis=0, concat_axis=0, tiled=True)


def pick(blocks, index):
    return lax.dynamic_index_in_dim(blocks, index, 0, keepdims=False)


def pieces_of(refs, at):
    return [r[:, at] for r in refs]


def start_kernel(*refs):
    rows_refs, weight_refs, pre_ref = refs[:4], refs[4:7], refs[7]
    for k, rows in enumerate(pieces_of(rows_refs, slice(None))):
        for j, weight in enumerate(weight_refs):
            pre_ref[j, k] = dot(rows, weight[:, :HALF], (1, 1))


def expert_kernel(*refs):
    rows_refs, (gate_ref, up_ref, down_ref) = refs[:4], refs[4:7]
    pre_ref, right_ref, back_refs = refs[7], refs[8], refs[9:]
    width = gate_ref.shape[0]
    wide = back_refs[0].shape[1]
    for k, rows in enumerate(pieces_of(rows_refs, slice(None))):
        block = rows.shape[0]
        place = lax.rem(lax.broadcasted_iota(jnp.int32, (block, width), 0), 2 * CAP)
        first = place < CAP
        gate_pre = pre_ref[0, k] + dot(rows, gate_ref[:, HALF:], (1, 1))
        up_pre = pre_ref[1, k] + dot(rows, up_ref[:, HALF:], (1, 1))
        hidden_grad = pre_ref[2, k] + dot(rows, down_ref[:, HALF:], (1, 1))
        hidden_grad = pltpu.roll(hidden_grad, block - CAP, 0)
        sig_gate = 1.0 / (1.0 + jnp.exp(-gate_pre))
        act_gate = gate_pre * sig_gate
        hidden = (act_gate * up_pre).astype(BF).astype(F32)
        slope = sig_gate * (1.0 + gate_pre * (1.0 - sig_gate))
        grad_gate = jnp.where(first, hidden_grad * up_pre * slope, 0.0)
        grad_up = jnp.where(first, hidden_grad * act_gate, 0.0)
        hidden = jnp.where(first, hidden, 0.0)
        comb = jnp.sum(hidden * hidden_grad, axis=1, keepdims=True)
        gate_lo, up_lo = grad_gate.astype(BF), grad_up.astype(BF)
        gate_hi, up_hi = pltpu.roll(grad_gate, CAP, 0).astype(BF), pltpu.roll(grad_up, CAP, 0).astype(BF)
        right_ref[k, :, :width] = gate_lo
        right_ref[k, :, width : 2 * width] = up_lo
        right_ref[k, :, 2 * width :] = pltpu.roll(hidden, CAP, 0).astype(BF)
        back = dot(gate_lo, gate_ref[:, :HALF], (1, 0)) + dot(up_lo, up_ref[:, :HALF], (1, 0))
        back = back + dot(gate_hi, gate_ref[:, HALF:], (1, 0)) + dot(up_hi, up_ref[:, HALF:], (1, 0))
        back_refs[k][:, :HALF] = back.astype(BF)
        back_refs[k][:, HALF:] = jnp.broadcast_to(comb, (block, wide - HALF)).astype(BF)


VMEM = pl.BlockSpec(memory_space=pltpu.VMEM)
SMEM = pl.BlockSpec(memory_space=pltpu.SMEM)


def start_pass(rows, weights):
    block, width = rows[0].shape[0], weights[0].shape[0]
    return pl.pallas_call(
        start_kernel,
        out_shape=jax.ShapeDtypeStruct((3, HSPLIT, block, width), F32),
        in_specs=[VMEM] * 7,
        out_specs=VMEM,
        cost_estimate=pl.CostEstimate(
            flops=2 * HSPLIT * block * HALF * 3 * width, bytes_accessed=5 << 20, transcendentals=0
        ),
    )(*rows, *weights)


def expert_pass(rows, weights, pre):
    block, width = rows[0].shape[0], weights[0].shape[0]
    return pl.pallas_call(
        expert_kernel,
        out_shape=(
            jax.ShapeDtypeStruct((HSPLIT, block, 3 * width), BF),
            *[jax.ShapeDtypeStruct((block, HALF + 128), BF)] * HSPLIT,
        ),
        in_specs=[VMEM] * 8,
        out_specs=[VMEM] * 5,
        cost_estimate=pl.CostEstimate(
            flops=2 * HSPLIT * block * HALF * 7 * width,
            bytes_accessed=10 << 20,
            transcendentals=HSPLIT * block * width,
        ),
    )(*rows, *weights, pre)


def term_kernel(n_c, core_ref, *refs):
    low_refs, high_refs, right_ref = refs[:4], refs[4:8], refs[8]
    mine_ref, theirs_ref = refs[9:]
    n_y, _, share = mine_ref.shape[:3]
    block, width = right_ref.shape[1:]
    right = right_ref[...].reshape(HSPLIT * block, width)
    even = core_ref[0] == 0
    group = n_c * share
    step = max(group, D // 4)
    for start in range(0, D, step):
        refs_now = low_refs if start < HALF else high_refs
        here = start % HALF
        rows = jnp.concatenate(pieces_of(refs_now, slice(here, here + step)), axis=0)
        term = dot(rows, right, (0, 0)).astype(BF)
        for g in range(step // group):
            place = start // group + g
            h, y = place // n_y, place % n_y
            zero = term[g * group : g * group + share]
            one = term[g * group + share : (g + 1) * group]
            mine_ref[y, h] = jnp.where(even, zero, one)
            theirs_ref[y, h] = jnp.where(even, one, zero)


def term_pass(core, low, high, right, n_h, n_y, n_c):
    share = D // (n_h * n_y * n_c)
    shape = jax.ShapeDtypeStruct((n_y, n_h, share, right.shape[2]), BF)
    return pl.pallas_call(
        functools.partial(term_kernel, n_c),
        out_shape=(shape, shape),
        in_specs=[SMEM] + [VMEM] * 9,
        out_specs=[VMEM] * 2,
        cost_estimate=pl.CostEstimate(
            flops=2 * HSPLIT * right.shape[1] * D * right.shape[2], bytes_accessed=8 << 20, transcendentals=0
        ),
    )(core, *low, *high, right)


def share_rows(own):
    rows = [own] + [flip(own, "x", k) for k in range(1, HSPLIT)]
    return [v.reshape(-1, v.shape[2]) for v in rows]


def local(tokens, out_grad, expert_ids, combine, w_gate, w_up, w_down):
    n_z = lax.axis_size("zl")
    tok_dev = tokens.shape[0]
    width = w_gate.shape[2]
    wanted = lax.broadcasted_iota(jnp.int32, (1, 1, n_z), 2)
    chosen = expert_ids[:, :, None] == wanted
    routed = jnp.any(chosen, axis=1).astype(jnp.int32)
    earlier = jnp.cumsum(routed, axis=0, dtype=jnp.int32) - routed
    slot_ids = lax.broadcasted_iota(jnp.int32, (1, CAP, 1), 1)
    picker = (earlier.T[:, None, :] == slot_ids) & (routed.T[:, None, :] == 1)
    weight_te = jnp.sum(jnp.where(chosen, combine[:, :, None], 0.0), axis=1)
    slot_w = jnp.sum(jnp.where(picker, weight_te.T[:, None, :], 0.0), axis=2)
    picker_bf = picker.astype(BF)
    blank = jnp.zeros_like(picker_bf)
    pick_x = jnp.concatenate([picker_bf, blank], axis=1).reshape(-1, tok_dev)
    pick_g = jnp.concatenate([blank, picker_bf], axis=1).reshape(-1, tok_dev)
    scale = jnp.concatenate([jnp.ones_like(slot_w), slot_w], axis=1).reshape(-1, 1)
    n_h, n_y, n_c = lax.axis_size("zh"), lax.axis_size("y"), lax.axis_size("c")
    weights = (w_gate[0].T, w_up[0].T, w_down[0])

    def send_rows(at):
        rows = dot(pick_x, tokens[:, at], (1, 0)) + dot(pick_g, out_grad[:, at], (1, 0))
        return exchange((rows * scale).astype(BF).reshape(n_z, 2 * CAP, HALF), "zl")

    low = share_rows(send_rows(slice(0, HALF)))
    high = share_rows(send_rows(slice(HALF, D)))
    pre = start_pass(low, weights)
    right, *back = expert_pass(high, weights, pre)

    core = lax.axis_index("c").reshape(1)
    mine, theirs = term_pass(core, low, high, right, n_h, n_y, n_c)
    others = flip(theirs, "c", 1)
    pair = (mine.astype(F32) + others.astype(F32)).astype(BF)
    line = exchange(pair, "y")
    line = jnp.sum(line.astype(F32), axis=0)
    high_at = lax.axis_index("zh")
    away = flip(pick(line, 1 - high_at).astype(BF), "zh", 1)
    summed = pick(line, high_at).astype(BF).astype(F32) + away.astype(F32)
    weight_grads = summed.astype(BF).reshape(1, -1, 3, width)

    total = back[0].astype(F32)
    for k in range(1, HSPLIT):
        other = flip(back[k], "x", k)
        total = total + other.astype(F32)
    ret = exchange(total.astype(BF).reshape(n_z, 2 * CAP, HALF + 128), "zl")

    flat_ret = ret.reshape(n_z * 2 * CAP, -1)[:, :HALF]
    grad_tokens = jnp.concatenate(
        [dot(pick_x, flat_ret, (0, 0)), dot(pick_g, flat_ret, (0, 0))], axis=1
    ).astype(BF)
    comb_slots = ret[:, :CAP, HALF].astype(F32)
    comb_te = jnp.sum(jnp.where(picker, comb_slots[:, :, None], 0.0), axis=1)
    raw = jnp.sum(jnp.where(chosen, comb_te.T[:, None, :], 0.0), axis=2)
    here = jnp.any(chosen, axis=2)
    grad_combine = jnp.where(here, raw / jnp.where(here, combine, 1.0), 0.0)
    return (grad_tokens, grad_combine, weight_grads)


def solution(mesh):
    n_expert, n_seq = mesh.devices.shape
    grid = Mesh(
        mesh.devices.reshape(n_expert // HSPLIT, HSPLIT, 2, n_seq // 4, 2),
        ("zl", "x", "zh", "y", "c"),
    )
    expert, seq = ("zl", "x"), ("zh", "y", "c")
    tok = P(expert + seq, None)
    wgt = P(expert, None, None)
    return jax.shard_map(
        local,
        mesh=grid,
        in_specs=(tok, tok, tok, tok, wgt, wgt, wgt),
        out_specs=(tok, tok, P(expert, seq, None, None)),
        check_vma=False,
    )
```

```python
import functools

import jax
import jax.numpy as jnp
from jax import lax
from jax.experimental import pallas as pl
from jax.experimental.pallas import tpu as pltpu
from jax.sharding import Mesh
from jax.sharding import PartitionSpec as P

D = 2048
HALF = 1024
HSPLIT = 4
CAP = 12
BF = jnp.bfloat16
F32 = jnp.float32


def dot(left, right, dims):
    return lax.dot_general(left, right, ((dims[:1], dims[1:]), ((), ())), preferred_element_type=F32)


def flip(values, axis, mask):
    size = lax.axis_size(axis)
    return lax.ppermute(values, axis, [(i, i ^ mask) for i in range(size)])


def exchange(values, axis):
    return lax.all_to_all(values, axis, split_axis=0, concat_axis=0, tiled=True)


def pick(blocks, index):
    return lax.dynamic_index_in_dim(blocks, index, 0, keepdims=False)


def hop_on(values):
    n = lax.axis_size("y")
    pairs = [(2 * i + c, 2 * ((i + (1, -1)[c]) % n) + c) for i in range(n) for c in range(2)]
    return lax.ppermute(values, ("y", "c"), pairs)


def ring_sum(mine, others):
    core = lax.axis_index("c")
    far = mine.shape[0]

    def at(blocks, step):
        return pick(blocks, jnp.where(core == 0, far - 1 - step, max(step - 1, 0))).astype(F32)

    first = jnp.where(core == 0, at(mine, 0) + at(others, 0), 0.0).astype(BF)
    run = hop_on(first)
    pair = (mine.astype(F32) + others.astype(F32)).astype(BF)
    for step in range(1, far):
        part = (at(pair, step) + run.astype(F32)).astype(BF)
        run = hop_on(part)
    run = run.astype(F32) + jnp.where(core == 0, 0.0, pair[far - 1].astype(F32))
    got = flip(pick(run, 1 - core).astype(BF), "c", 1)
    return pick(run, core) + got.astype(F32)


def forward(rows, weight_refs, at):
    return [dot(rows, weight[:, at], (1, 1)) for weight in weight_refs]


def start_kernel(*refs):
    rows_refs, weight_refs, pre_ref = refs[:4], refs[4:7], refs[7]
    rows = jnp.concatenate([r[...] for r in rows_refs], axis=0)
    for j, value in enumerate(forward(rows, weight_refs, slice(0, HALF))):
        pre_ref[j] = value


def expert_kernel(me_ref, *refs):
    rows_refs, (gate_ref, up_ref, down_ref, pre_ref, right_ref, back_ref) = refs[:4], refs[4:]
    width = gate_ref.shape[0]
    block = rows_refs[0].shape[0]
    me = me_ref[0]
    rows = jnp.concatenate([r[...] for r in rows_refs], axis=0)
    done = forward(rows, (gate_ref, up_ref, down_ref), slice(HALF, D))
    place = lax.rem(lax.broadcasted_iota(jnp.int32, (block, width), 0), 2 * CAP)
    first = place < CAP
    lefts, combs = [[], [], [], []], []
    for k in range(HSPLIT):
        at = slice(k * block, (k + 1) * block)
        gate_pre, up_pre, hidden_grad = [pre_ref[j, at] + done[j][at] for j in range(3)]
        hidden_grad = pltpu.roll(hidden_grad, block - CAP, 0)
        sig_gate = 1.0 / (1.0 + jnp.exp(-gate_pre))
        act_gate = gate_pre * sig_gate
        hidden = (act_gate * up_pre).astype(BF).astype(F32)
        slope = sig_gate * (1.0 + gate_pre * (1.0 - sig_gate))
        grad_gate = jnp.where(first, hidden_grad * up_pre * slope, 0.0)
        grad_up = jnp.where(first, hidden_grad * act_gate, 0.0)
        hidden = jnp.where(first, hidden, 0.0)
        combs.append(jnp.sum(hidden * hidden_grad, axis=1, keepdims=True))
        both = (grad_gate, grad_up, pltpu.roll(grad_gate, CAP, 0), pltpu.roll(grad_up, CAP, 0))
        for left, value in zip(lefts, both):
            left.append(value.astype(BF))
        right_ref[k, :, :width] = lefts[0][k]
        right_ref[k, :, width : 2 * width] = lefts[1][k]
        right_ref[k, :, 2 * width :] = pltpu.roll(hidden, CAP, 0).astype(BF)
    left = [jnp.concatenate(v, axis=0) for v in lefts]
    step = HALF // 2
    for start in range(0, HALF, step):
        lo, hi = slice(start, start + step), slice(HALF + start, HALF + start + step)
        back = dot(left[0], gate_ref[:, lo], (1, 0)) + dot(left[1], up_ref[:, lo], (1, 0))
        back = back + dot(left[2], gate_ref[:, hi], (1, 0)) + dot(left[3], up_ref[:, hi], (1, 0))
        for k in range(HSPLIT):
            for z in range(block // (2 * CAP)):
                for i in range(3):
                    row = k * block + z * 2 * CAP + i * 8
                    there = slice(i * HALF + start, i * HALF + start + step)
                    back_ref[lax.bitwise_xor(me, k), z, :, there] = back[row : row + 8].astype(BF)
    for k in range(HSPLIT):
        wide = jnp.broadcast_to(combs[k], (block, 128))
        left_lanes = lax.broadcasted_iota(jnp.int32, (8, 128), 1) < 64
        for z in range(block // (2 * CAP)):
            row = z * 2 * CAP
            side = jnp.where(left_lanes, wide[row : row + 8], wide[row + 8 : row + 16])
            back_ref[lax.bitwise_xor(me, k), z, :, 3 * HALF :] = side.astype(BF)


VMEM = pl.BlockSpec(memory_space=pltpu.VMEM)
SMEM = pl.BlockSpec(memory_space=pltpu.SMEM)


def start_pass(rows, weights):
    block, width = rows[0].shape[0], weights[0].shape[0]
    return pl.pallas_call(
        start_kernel,
        out_shape=jax.ShapeDtypeStruct((3, HSPLIT * block, width), F32),
        in_specs=[VMEM] * 7,
        out_specs=VMEM,
        cost_estimate=pl.CostEstimate(
            flops=2 * HSPLIT * block * HALF * 3 * width, bytes_accessed=5 << 20, transcendentals=0
        ),
    )(*rows, *weights)


def expert_pass(me, rows, weights, pre):
    block, width = rows[0].shape[0], weights[0].shape[0]
    n_z = block // (2 * CAP)
    return pl.pallas_call(
        expert_kernel,
        out_shape=(
            jax.ShapeDtypeStruct((HSPLIT, block, 3 * width), BF),
            jax.ShapeDtypeStruct((HSPLIT, n_z, 8, 3 * HALF + 128), BF),
        ),
        in_specs=[SMEM] + [VMEM] * 8,
        out_specs=[VMEM] * 2,
        cost_estimate=pl.CostEstimate(
            flops=2 * HSPLIT * block * HALF * 7 * width,
            bytes_accessed=10 << 20,
            transcendentals=HSPLIT * block * width,
        ),
    )(me, *rows, *weights, pre)


def term_kernel(n_h, at_ref, *refs):
    low_refs, high_refs, (right_ref, out_ref) = refs[:4], refs[4:8], refs[8:]
    n_y, n_c, share = out_ref.shape[:3]
    width = right_ref.shape[2]
    main = width // 128 * 128
    rest = width - main
    core, me = at_ref[0], at_ref[1]
    group = n_c * share
    step = max(group, D // 4)
    right = right_ref[...].reshape(-1, width)
    for half in range(2):
        for start in range(0, HALF, step):
            now = slice(start, start + step)
            rows = jnp.concatenate([r[:, now] for r in (low_refs, high_refs)[half]], axis=0)
            term = dot(rows, right, (0, 0)).astype(BF)
            for g in range(step // group):
                place = (half * HALF + start) // group + g
                h, y = place // n_y, place % n_y
                spot = lax.rem(y - me - 1 + 2 * n_y + core * (n_y // 2), n_y)
                tail = slice(n_h * main + h * rest, n_h * main + (h + 1) * rest)
                for c in range(n_c):
                    block = term[g * group + c * share : g * group + (c + 1) * share]
                    out_ref[spot, c, :, h * main : (h + 1) * main] = block[:, :main]
                    out_ref[spot, c, :, tail] = block[:, main:]


def term_pass(at, low, high, right, n_h, n_y, n_c):
    share = D // (n_h * n_y * n_c)
    return pl.pallas_call(
        functools.partial(term_kernel, n_h),
        out_shape=jax.ShapeDtypeStruct((n_y, n_c, share, n_h * right.shape[2]), BF),
        in_specs=[SMEM] + [VMEM] * 9,
        out_specs=VMEM,
        cost_estimate=pl.CostEstimate(
            flops=2 * HSPLIT * right.shape[1] * D * right.shape[2], bytes_accessed=8 << 20, transcendentals=0
        ),
    )(at, *low, *high, right)


def share_rows(own):
    rows = [own]
    for k in range(1, HSPLIT):
        rows.append(flip(own, "x", k))
    return [v.reshape(-1, v.shape[2]) for v in rows]


def local(tokens, out_grad, expert_ids, combine, w_gate, w_up, w_down):
    n_z = lax.axis_size("zl")
    tok_dev = tokens.shape[0]
    width = w_gate.shape[2]
    wanted = lax.broadcasted_iota(jnp.int32, (1, 1, n_z), 2)
    chosen = expert_ids[:, :, None] == wanted
    routed = jnp.any(chosen, axis=1).astype(jnp.int32)
    earlier = jnp.cumsum(routed, axis=0, dtype=jnp.int32) - routed
    slot_ids = lax.broadcasted_iota(jnp.int32, (1, CAP, 1), 1)
    picker = (earlier.T[:, None, :] == slot_ids) & (routed.T[:, None, :] == 1)
    weight_te = jnp.sum(jnp.where(chosen, combine[:, :, None], 0.0), axis=1)
    slot_w = jnp.sum(jnp.where(picker, weight_te.T[:, None, :], 0.0), axis=2)
    picker_bf = picker.astype(BF)
    blank = jnp.zeros_like(picker_bf)
    pick_x = jnp.concatenate([picker_bf, blank], axis=1).reshape(-1, tok_dev)
    pick_g = jnp.concatenate([blank, picker_bf], axis=1).reshape(-1, tok_dev)
    scale = jnp.concatenate([jnp.ones_like(slot_w), slot_w], axis=1).reshape(-1, 1)
    n_h, n_y, n_c = lax.axis_size("zh"), lax.axis_size("y"), lax.axis_size("c")
    weights = (w_gate[0].T, w_up[0].T, w_down[0])

    def send_rows(at):
        rows = dot(pick_x, tokens[:, at], (1, 0)) + dot(pick_g, out_grad[:, at], (1, 0))
        return exchange((rows * scale).astype(BF).reshape(n_z, 2 * CAP, HALF), "zl")

    low = share_rows(send_rows(slice(0, HALF)))
    own = send_rows(slice(HALF, D))
    high = share_rows(own)
    pre = start_pass(low, weights)
    me = lax.axis_index("x")
    right, back = expert_pass(me.reshape(1), high, weights, pre)

    at = jnp.stack([lax.axis_index("c"), lax.axis_index("y")])
    terms = term_pass(at, low, high, right, n_h, n_y, n_c)
    mine, theirs = terms[: n_y // 2], terms[n_y // 2 :]
    others = flip(theirs, "c", 1)
    line = ring_sum(mine, others).astype(BF)
    wide = 3 * width // 128 * 128
    ends = [
        jnp.concatenate(
            [
                line[:, h * wide : (h + 1) * wide],
                line[:, n_h * wide + h * (3 * width - wide) :][:, : 3 * width - wide],
            ],
            axis=1,
        )
        for h in range(n_h)
    ]
    low_half = lax.axis_index("zh") == 0
    away = flip(jnp.where(low_half, ends[1], ends[0]), "zh", 1)
    summed = jnp.where(low_half, ends[0], ends[1]).astype(F32) + away.astype(F32)
    weight_grads = summed.astype(BF).reshape(1, -1, 3, width)

    back = exchange(back, "x")
    total = jnp.sum(back.astype(F32), axis=0)
    ret = exchange(total.astype(BF), "zl")

    def by_tile(picks):
        return picks.reshape(n_z, 3, 8, tok_dev).transpose(1, 0, 2, 3).reshape(-1, tok_dev)

    rows_back = jnp.concatenate(
        [ret[:, :, i * HALF : (i + 1) * HALF].reshape(n_z * 8, HALF) for i in range(3)], axis=0
    )
    grad_tokens = jnp.concatenate(
        [dot(by_tile(pick_x), rows_back, (0, 0)), dot(by_tile(pick_g), rows_back, (0, 0))], axis=1
    ).astype(BF)
    side = ret[:, :, 3 * HALF :].astype(F32)
    comb_slots = jnp.concatenate([side[:, :, 0], side[:, : CAP - 8, 64]], axis=1)
    comb_te = jnp.sum(jnp.where(picker, comb_slots[:, :, None], 0.0), axis=1)
    raw = jnp.sum(jnp.where(chosen, comb_te.T[:, None, :], 0.0), axis=2)
    here = jnp.any(chosen, axis=2)
    grad_combine = jnp.where(here, raw / jnp.where(here, combine, 1.0), 0.0)
    return (grad_tokens, grad_combine, weight_grads)


def solution(mesh):
    n_expert, n_seq = mesh.devices.shape
    grid = Mesh(
        mesh.devices.reshape(n_expert // HSPLIT, HSPLIT, 2, n_seq // 4, 2),
        ("zl", "x", "zh", "y", "c"),
    )
    expert, seq = ("zl", "x"), ("zh", "y", "c")
    tok = P(expert + seq, None)
    wgt = P(expert, None, None)
    return jax.shard_map(
        local,
        mesh=grid,
        in_specs=(tok, tok, tok, tok, wgt, wgt, wgt),
        out_specs=(tok, tok, P(expert, seq, None, None)),
        check_vma=False,
    )
```

```python
import functools

import jax
import jax.numpy as jnp
from jax import lax
from jax.experimental import pallas as pl
from jax.experimental.pallas import tpu as pltpu
from jax.sharding import Mesh
from jax.sharding import PartitionSpec as P

D = 2048
HALF = 1024
HSPLIT = 4
CAP = 12
BF = jnp.bfloat16
F32 = jnp.float32


def dot(left, right, dims):
    return lax.dot_general(left, right, ((dims[:1], dims[1:]), ((), ())), preferred_element_type=F32)


def flip(values, axis, mask):
    size = lax.axis_size(axis)
    return lax.ppermute(values, axis, [(i, i ^ mask) for i in range(size)])


def exchange(values, axis):
    return lax.all_to_all(values, axis, split_axis=0, concat_axis=0, tiled=True)


def pick(blocks, index):
    return lax.dynamic_index_in_dim(blocks, index, 0, keepdims=False)


def shift(values, axis, step):
    size = lax.axis_size(axis)
    return lax.ppermute(values, axis, [(i, (i + step) % size) for i in range(size)])


def ring_sum(mine, others):
    n = lax.axis_size("y")
    me = lax.axis_index("y")
    far = n // 2

    def at(blocks, step):
        return pick(blocks, lax.rem(me + step + n, n)).astype(F32)

    first = (at(mine, far) + at(others, far)).astype(BF)
    up = shift(first, "y", 1)
    pair = (mine.astype(F32) + others.astype(F32)).astype(BF)
    down = None
    for hop in range(far - 1, 0, -1):
        up_part = (at(pair, hop) + up.astype(F32)).astype(BF)
        down_part = at(pair, -hop)
        if down is not None:
            down_part = down_part + down.astype(F32)
        up = shift(up_part, "y", 1)
        down = shift(down_part.astype(BF), "y", -1)
        up, down = lax.optimization_barrier((up, down))
    total = at(pair, 0) + up.astype(F32)
    return total if down is None else total + down.astype(F32)


def forward(rows, weight_refs, at):
    return [dot(rows, weight[:, at], (1, 1)) for weight in weight_refs]


def start_kernel(*refs):
    rows_refs, weight_refs, pre_ref = refs[:4], refs[4:7], refs[7]
    rows = jnp.concatenate([r[...] for r in rows_refs], axis=0)
    for j, value in enumerate(forward(rows, weight_refs, slice(0, HALF))):
        pre_ref[j] = value


def expert_kernel(me_ref, *refs):
    rows_refs, (gate_ref, up_ref, down_ref, pre_ref, right_ref, back_ref) = refs[:4], refs[4:]
    width = gate_ref.shape[0]
    block = rows_refs[0].shape[0]
    me = me_ref[0]
    rows = jnp.concatenate([r[...] for r in rows_refs], axis=0)
    done = forward(rows, (gate_ref, up_ref, down_ref), slice(HALF, D))
    place = lax.rem(lax.broadcasted_iota(jnp.int32, (block, width), 0), 2 * CAP)
    first = place < CAP
    lefts, combs = [[], [], [], []], []
    for k in range(HSPLIT):
        at = slice(k * block, (k + 1) * block)
        gate_pre, up_pre, hidden_grad = [pre_ref[j, at] + done[j][at] for j in range(3)]
        hidden_grad = pltpu.roll(hidden_grad, block - CAP, 0)
        sig_gate = 1.0 / (1.0 + jnp.exp(-gate_pre))
        act_gate = gate_pre * sig_gate
        hidden = (act_gate * up_pre).astype(BF).astype(F32)
        slope = sig_gate * (1.0 + gate_pre * (1.0 - sig_gate))
        grad_gate = jnp.where(first, hidden_grad * up_pre * slope, 0.0)
        grad_up = jnp.where(first, hidden_grad * act_gate, 0.0)
        hidden = jnp.where(first, hidden, 0.0)
        combs.append(jnp.sum(hidden * hidden_grad, axis=1, keepdims=True))
        both = (grad_gate, grad_up, pltpu.roll(grad_gate, CAP, 0), pltpu.roll(grad_up, CAP, 0))
        for left, value in zip(lefts, both):
            left.append(value.astype(BF))
        right_ref[k, :, :width] = lefts[0][k]
        right_ref[k, :, width : 2 * width] = lefts[1][k]
        right_ref[k, :, 2 * width :] = pltpu.roll(hidden, CAP, 0).astype(BF)
    left = [jnp.concatenate(v, axis=0) for v in lefts]
    step = HALF // 2
    for start in range(0, HALF, step):
        lo, hi = slice(start, start + step), slice(HALF + start, HALF + start + step)
        back = dot(left[0], gate_ref[:, lo], (1, 0)) + dot(left[1], up_ref[:, lo], (1, 0))
        back = back + dot(left[2], gate_ref[:, hi], (1, 0)) + dot(left[3], up_ref[:, hi], (1, 0))
        for k in range(HSPLIT):
            for z in range(block // (2 * CAP)):
                for i in range(3):
                    row = k * block + z * 2 * CAP + i * 8
                    there = slice(i * HALF + start, i * HALF + start + step)
                    back_ref[lax.bitwise_xor(me, k), z, :, there] = back[row : row + 8].astype(BF)
    for k in range(HSPLIT):
        wide = jnp.broadcast_to(combs[k], (block, 128))
        left_lanes = lax.broadcasted_iota(jnp.int32, (8, 128), 1) < 64
        for z in range(block // (2 * CAP)):
            row = z * 2 * CAP
            side = jnp.where(left_lanes, wide[row : row + 8], wide[row + 8 : row + 16])
            back_ref[lax.bitwise_xor(me, k), z, :, 3 * HALF :] = side.astype(BF)


VMEM = pl.BlockSpec(memory_space=pltpu.VMEM)
SMEM = pl.BlockSpec(memory_space=pltpu.SMEM)


def start_pass(rows, weights):
    block, width = rows[0].shape[0], weights[0].shape[0]
    return pl.pallas_call(
        start_kernel,
        out_shape=jax.ShapeDtypeStruct((3, HSPLIT * block, width), F32),
        in_specs=[VMEM] * 7,
        out_specs=VMEM,
        cost_estimate=pl.CostEstimate(
            flops=2 * HSPLIT * block * HALF * 3 * width, bytes_accessed=5 << 20, transcendentals=0
        ),
    )(*rows, *weights)


def expert_pass(me, rows, weights, pre):
    block, width = rows[0].shape[0], weights[0].shape[0]
    n_z = block // (2 * CAP)
    return pl.pallas_call(
        expert_kernel,
        out_shape=(
            jax.ShapeDtypeStruct((HSPLIT, block, 3 * width), BF),
            jax.ShapeDtypeStruct((HSPLIT, n_z, 8, 3 * HALF + 128), BF),
        ),
        in_specs=[SMEM] + [VMEM] * 8,
        out_specs=[VMEM] * 2,
        cost_estimate=pl.CostEstimate(
            flops=2 * HSPLIT * block * HALF * 7 * width,
            bytes_accessed=10 << 20,
            transcendentals=HSPLIT * block * width,
        ),
    )(me, *rows, *weights, pre)


def term_kernel(n_h, n_c, at_ref, *refs):
    low_refs, high_refs, (right_ref, mine_ref, theirs_ref) = refs[:4], refs[4:8], refs[8:]
    n_y, share = mine_ref.shape[:2]
    width = right_ref.shape[2]
    main = width // 128 * 128
    rest = width - main
    even = at_ref[0] == 0
    group = n_c * share
    step = max(group, D // 4)
    right = right_ref[...].reshape(-1, width)
    for half in range(2):
        for start in range(0, HALF, step):
            now = slice(start, start + step)
            rows = jnp.concatenate([r[:, now] for r in (low_refs, high_refs)[half]], axis=0)
            term = dot(rows, right, (0, 0)).astype(BF)
            for g in range(step // group):
                place = (half * HALF + start) // group + g
                h, y = place // n_y, place % n_y
                zero = term[g * group : g * group + share]
                one = term[g * group + share : (g + 1) * group]
                tail = slice(n_h * main + h * rest, n_h * main + (h + 1) * rest)
                for ref, block in ((mine_ref, jnp.where(even, zero, one)), (theirs_ref, jnp.where(even, one, zero))):
                    ref[y, :, h * main : (h + 1) * main] = block[:, :main]
                    ref[y, :, tail] = block[:, main:]


def term_pass(at, low, high, right, n_h, n_y, n_c):
    share = D // (n_h * n_y * n_c)
    shape = jax.ShapeDtypeStruct((n_y, share, n_h * right.shape[2]), BF)
    return pl.pallas_call(
        functools.partial(term_kernel, n_h, n_c),
        out_shape=(shape, shape),
        in_specs=[SMEM] + [VMEM] * 9,
        out_specs=[VMEM] * 2,
        cost_estimate=pl.CostEstimate(
            flops=2 * HSPLIT * right.shape[1] * D * right.shape[2], bytes_accessed=8 << 20, transcendentals=0
        ),
    )(at, *low, *high, right)


def share_rows(own):
    rows = [own]
    for k in range(1, HSPLIT):
        rows.append(flip(own, "x", k))
    return [v.reshape(-1, v.shape[2]) for v in rows]


def local(tokens, out_grad, expert_ids, combine, w_gate, w_up, w_down):
    n_z = lax.axis_size("zl")
    tok_dev = tokens.shape[0]
    width = w_gate.shape[2]
    wanted = lax.broadcasted_iota(jnp.int32, (1, 1, n_z), 2)
    chosen = expert_ids[:, :, None] == wanted
    routed = jnp.any(chosen, axis=1).astype(jnp.int32)
    earlier = jnp.cumsum(routed, axis=0, dtype=jnp.int32) - routed
    slot_ids = lax.broadcasted_iota(jnp.int32, (1, CAP, 1), 1)
    picker = (earlier.T[:, None, :] == slot_ids) & (routed.T[:, None, :] == 1)
    weight_te = jnp.sum(jnp.where(chosen, combine[:, :, None], 0.0), axis=1)
    slot_w = jnp.sum(jnp.where(picker, weight_te.T[:, None, :], 0.0), axis=2)
    picker_bf = picker.astype(BF)
    blank = jnp.zeros_like(picker_bf)
    pick_x = jnp.concatenate([picker_bf, blank], axis=1).reshape(-1, tok_dev)
    pick_g = jnp.concatenate([blank, picker_bf], axis=1).reshape(-1, tok_dev)
    scale = jnp.concatenate([jnp.ones_like(slot_w), slot_w], axis=1).reshape(-1, 1)
    n_h, n_y, n_c = lax.axis_size("zh"), lax.axis_size("y"), lax.axis_size("c")
    weights = (w_gate[0].T, w_up[0].T, w_down[0])

    def send_rows(at):
        rows = dot(pick_x, tokens[:, at], (1, 0)) + dot(pick_g, out_grad[:, at], (1, 0))
        return exchange((rows * scale).astype(BF).reshape(n_z, 2 * CAP, HALF), "zl")

    low = share_rows(send_rows(slice(0, HALF)))
    own = send_rows(slice(HALF, D))
    high = share_rows(own)
    pre = start_pass(low, weights)
    me = lax.axis_index("x")
    right, back = expert_pass(me.reshape(1), high, weights, pre)

    at = lax.axis_index("c").reshape(1)
    mine, theirs = term_pass(at, low, high, right, n_h, n_y, n_c)
    others = flip(theirs, "c", 1)
    line = ring_sum(mine, others).astype(BF)
    wide = 3 * width // 128 * 128
    ends = [
        jnp.concatenate(
            [
                line[:, h * wide : (h + 1) * wide],
                line[:, n_h * wide + h * (3 * width - wide) :][:, : 3 * width - wide],
            ],
            axis=1,
        )
        for h in range(n_h)
    ]
    low_half = lax.axis_index("zh") == 0
    away = flip(jnp.where(low_half, ends[1], ends[0]), "zh", 1)
    summed = jnp.where(low_half, ends[0], ends[1]).astype(F32) + away.astype(F32)
    weight_grads = summed.astype(BF).reshape(1, -1, 3, width)

    back = exchange(back, "x")
    total = jnp.sum(back.astype(F32), axis=0)
    ret = exchange(total.astype(BF), "zl")

    def by_tile(picks):
        return picks.reshape(n_z, 3, 8, tok_dev).transpose(1, 0, 2, 3).reshape(-1, tok_dev)

    rows_back = jnp.concatenate(
        [ret[:, :, i * HALF : (i + 1) * HALF].reshape(n_z * 8, HALF) for i in range(3)], axis=0
    )
    grad_tokens = jnp.concatenate(
        [dot(by_tile(pick_x), rows_back, (0, 0)), dot(by_tile(pick_g), rows_back, (0, 0))], axis=1
    ).astype(BF)
    side = ret[:, :, 3 * HALF :].astype(F32)
    comb_slots = jnp.concatenate([side[:, :, 0], side[:, : CAP - 8, 64]], axis=1)
    comb_te = jnp.sum(jnp.where(picker, comb_slots[:, :, None], 0.0), axis=1)
    raw = jnp.sum(jnp.where(chosen, comb_te.T[:, None, :], 0.0), axis=2)
    here = jnp.any(chosen, axis=2)
    grad_combine = jnp.where(here, raw / jnp.where(here, combine, 1.0), 0.0)
    return (grad_tokens, grad_combine, weight_grads)


def solution(mesh):
    n_expert, n_seq = mesh.devices.shape
    grid = Mesh(
        mesh.devices.reshape(n_expert // HSPLIT, HSPLIT, 2, n_seq // 4, 2),
        ("zl", "x", "zh", "y", "c"),
    )
    expert, seq = ("zl", "x"), ("zh", "y", "c")
    tok = P(expert + seq, None)
    wgt = P(expert, None, None)
    return jax.shard_map(
        local,
        mesh=grid,
        in_specs=(tok, tok, tok, tok, wgt, wgt, wgt),
        out_specs=(tok, tok, P(expert, seq, None, None)),
        check_vma=False,
    )
```
